512 devices in a mesh: vocab: 64 (over z, x_lo, core), hid: 8 (over x_hi, y).
Axes of the slice: x: 4 (x_hi: 2, x_lo: 2; x = x_hi * 2 + x_lo), y: 4, z: 16, core: 2. Of those that a mesh axis runs over, the one named last changes fastest.
Arguments:
- posterior: bfloat16 [512, 16384], P(None, 'vocab'), may hold values from 1.9e-09 to 1, as said below
- transition: bfloat16 [16384, 16384], P('vocab', 'hid'), may hold values from 1e-07 to 1, as said below
- emission: bfloat16 [16384, 16384], P('hid', 'vocab'), may hold values from 6e-06 to 90, as said below
- advance: bfloat16 [256, 16384], P(None, 'hid'), may hold values from 0.0099487305 to 1
- dfa_state: int32 [512], replicated, may hold values from 0 to 255
- edge_next: int32 [256, 8], replicated, may hold values from 0 to 255
- token_edge: int32 [256, 16384], P(None, 'vocab'), may hold values from 0 to 7
- allowed: int32 [512, 128], P(None, 'vocab'), may hold values from 0 to 1, as said below
Outputs:
- constrained_logprob: float32 [512, 16384], P('hid', 'vocab')
The draws below stay inside these ranges and needn't reach their ends.
Inputs may be any that keep to these rules, and one draw needn't show every extreme that they name: `allowed`: every request allows at least one block. `posterior`: positive. `transition`: positive. `emission`: positive.
All inputs are finite; a program needn't handle non-finite values.
Results may differ from the reference program's by a relative error of at most 0.0015.
Values may be sent and summed in bfloat16 or wider, within the bound.
A program may use at most 64 MiB of HBM per device.

```python
import math
import jax
import jax.numpy as jnp
from jax import lax

H = 16384
V = 16384
BLK = 128
S = 256
K = 8
R = 512
NB = 128


def draw_posterior(key, part):
    logs = 2.5 * jax.random.truncated_normal(key, -4.0, 4.0, (R, H), jnp.float32) - 10.0
    return jnp.exp(logs).astype(jnp.bfloat16)


def draw_transition(key, part):
    logs = 2.0 * jax.random.truncated_normal(key, -4.0, 4.0, (H, H), jnp.float32) - 8.0
    return jnp.exp(logs).astype(jnp.bfloat16)


def draw_emission(key, part):
    boost_key = jax.random.fold_in(key, 5)
    frequency_key = jax.random.fold_in(key, 7)
    logs = 1.5 * jax.random.truncated_normal(key, -4.0, 4.0, (H, V), jnp.float32) - 6.0
    frequency = jnp.exp(jax.random.uniform(frequency_key, (V,), jnp.float32, 0.0, math.log(3.0)))
    boost_table = jnp.exp(jax.random.uniform(boost_key, (16, NB), jnp.float32, 0.0, math.log(30.0)))
    row_group = jnp.arange(H, dtype=jnp.int32) * 16 // H
    column_block = jnp.arange(V, dtype=jnp.int32) // BLK
    boost = jnp.take(jnp.take(boost_table, row_group, axis=0), column_block, axis=1)
    return (jnp.exp(logs) * frequency[None, :] * boost).astype(jnp.bfloat16)


def draw_allowed(key, part):
    coin_key = jax.random.fold_in(key, 11)
    pick_key = jax.random.fold_in(key, 23)
    coins = jax.random.randint(coin_key, (R, NB), 0, 16)
    forced = jax.random.randint(pick_key, (R, 1), 0, NB)
    blocks = jnp.arange(NB, dtype=jnp.int32)[None, :]
    return jnp.where((coins == 0) | (blocks == forced), 1, 0).astype(jnp.int32)


def set_ends(result, stream_key, smallest, high):
    spot = [jax.random.randint(jax.random.fold_in(stream_key, axis), (), 0, length) for axis, length in enumerate(result.shape)]
    main_axis = result.shape.index(max(result.shape))
    next_to = spot[:main_axis] + [(spot[main_axis] + 1) % result.shape[main_axis]] + spot[main_axis + 1:]
    return result.at[tuple(spot)].set(smallest).at[tuple(next_to)].set(high)


def block_levels(own_key, dims, split, least, largest):
    level, own = 1.0, jax.random.fold_in(own_key, 6)
    for axis_at, shards_of in split:
        draws = jnp.exp(jax.random.uniform(jax.random.fold_in(own, axis_at), (shards_of,), jnp.float32, least / len(split), largest / len(split)))
        level = level * jnp.repeat(draws, dims[axis_at] // shards_of).reshape([-1 if axis == axis_at else 1 for axis in range(len(dims))])
    return level


def setup_inputs(seed: int = 0) -> dict:
    key_of = jax.random.split(jax.random.key(seed), 9)
    return {
        "posterior": draw_posterior(jax.random.fold_in(key_of[8], 71), 0),
        "transition": draw_transition(jax.random.fold_in(key_of[8], 71), 0),
        "emission": draw_emission(jax.random.fold_in(key_of[8], 71), 0),
        "advance": jnp.clip(jnp.exp(math.log(1.0) - 4.61031033 * jax.random.uniform(key_of[3], (S, H), jnp.float32) ** block_levels(key_of[3], (S, H), ((1, 8),), -0.2, 0.2)), 0.0099487305, 1.0).astype(jnp.bfloat16),
        "dfa_state": set_ends(jax.random.randint(key_of[4], (R,), 0, S), jax.random.fold_in(key_of[4], 1), 0, S - 1).astype(jnp.int32),
        "edge_next": set_ends(jax.random.randint(key_of[5], (S, K), 0, S), jax.random.fold_in(key_of[5], 1), 0, S - 1).astype(jnp.int32),
        "token_edge": set_ends(jax.random.randint(key_of[6], (S, V), 0, K), jax.random.fold_in(key_of[6], 1), 0, K - 1).astype(jnp.int32),
        "allowed": draw_allowed(jax.random.fold_in(key_of[8], 71), 0),
    }


def request_scores(prior_rows, first_row, dfa_state, edge_next, token_edge, allowed, advance, emission):
    row_count = prior_rows.shape[0]
    states = lax.dynamic_slice_in_dim(dfa_state, first_row, row_count, 0)
    successor = jnp.take(edge_next, states, axis=0)
    look_rows = jnp.take(advance, successor, axis=0)
    weighted = (prior_rows.astype(jnp.float32)[:, None, :] * look_rows.astype(jnp.float32)).astype(jnp.bfloat16)
    slot_count = successor.shape[1]
    flattened = weighted.reshape(row_count * slot_count, weighted.shape[2])
    candidate = jnp.dot(flattened, emission, preferred_element_type=jnp.float32).reshape(row_count, slot_count, emission.shape[1])
    edge_slots = jnp.take(token_edge, states, axis=0)
    labels = jnp.arange(slot_count, dtype=jnp.int32)
    chosen = jnp.sum(jnp.where(edge_slots[:, None, :] == labels[None, :, None], candidate, jnp.float32(0.0)), axis=1)
    mask_rows = lax.dynamic_slice_in_dim(allowed, first_row, row_count, 0)
    token_mask = jnp.repeat(mask_rows, BLK, axis=1)
    return jnp.where(token_mask > 0, chosen, jnp.float32(0.0))


def reference(posterior, transition, emission, advance, dfa_state, edge_next, token_edge, allowed):
    prior = jnp.dot(posterior, transition, preferred_element_type=jnp.float32).astype(jnp.bfloat16)
    block_rows = R // 8
    stacked = prior.reshape(8, block_rows, H)
    starts = jnp.arange(8, dtype=jnp.int32) * block_rows

    def one_block(operands):
        return request_scores(operands[0], operands[1], dfa_state, edge_next, token_edge, allowed, advance, emission)

    pieces = lax.map(one_block, (stacked, starts))
    scores = pieces.reshape(R, V)
    totals = jnp.sum(scores, axis=1)
    token_mask = jnp.repeat(allowed, BLK, axis=1) > 0
    safe = jnp.where(token_mask, scores, jnp.float32(1.0))
    return jnp.where(token_mask, jnp.log(safe) - jnp.log(totals)[:, None], jnp.float32(0.0))
```

```python
import jax
import jax.numpy as jnp
from jax import lax
from jax.experimental import pallas as pl
from jax.experimental.pallas import tpu as pltpu
from jax.sharding import PartitionSpec as P

MESH = pl.DeviceIdType.MESH
BF = jnp.bfloat16
F32 = jnp.float32
NZ = 16
CH = 16
HALF = 256
KC = 1024
TK = 256
MW = 384


def remote(src, dst, send, recv, a, b):
    return pltpu.make_async_remote_copy(
        src_ref=src,
        dst_ref=dst,
        send_sem=send,
        recv_sem=recv,
        device_id={"vocab": a, "hid": b},
        device_id_type=MESH,
    )


def kernel(
    post,
    trans,
    em,
    adv,
    dfa,
    edge,
    tedge,
    allow,
    out,
    csend,
    crecv,
    own,
    xsend,
    xrecv,
    zsend,
    zrecv,
    pri,
    em4,
    te_own,
    te4,
    gath,
    wbuf,
    cand,
    hsend,
    hrecv,
    tsend,
    trecv,
    s_c,
    r_c,
    s_x,
    r_x,
    s_z,
    r_z,
    s_g,
    r_g,
    s_e,
    r_e,
    s_t,
    r_t,
    s_h,
    r_h,
    s_s,
    r_s,
    l_e,
):
    a = lax.axis_index("vocab")
    b = lax.axis_index("hid")
    z = a // 4
    q = lax.rem(a, 4)
    xl = q // 2
    core = lax.rem(q, 2)
    ocore = 1 - core
    oxl = 1 - xl
    a_core = 4 * z + 2 * xl + ocore
    a_x = 4 * z + 2 * oxl + core
    a_d = 4 * z + 2 * oxl + ocore

    def zmod(v):
        return lax.rem(v + 2 * NZ, NZ)

    def z_dev(zz):
        return 4 * zz + q

    bar = pltpu.get_barrier_semaphore()

    def sig_group(i, c):
        m = lax.rem(q * 8 + b + i, 32)
        pl.semaphore_signal(
            bar, inc=1, device_id={"vocab": 4 * z + m // 8, "hid": lax.rem(m, 8)}, device_id_type=MESH
        )
        return c

    def sig_z(i, c):
        pl.semaphore_signal(
            bar, inc=1, device_id={"vocab": z_dev(zmod(z + i)), "hid": b}, device_id_type=MESH
        )
        return c

    lax.fori_loop(1, 32, sig_group, 0)
    lax.fori_loop(1, NZ, sig_z, 0)

    def part(row_half, col_half):
        rows = pl.ds(pl.multiple_of(row_half * HALF, HALF), HALF)
        cols = pl.ds(pl.multiple_of(col_half * KC, KC), KC)
        return jnp.dot(post[rows, :], trans[:, cols], preferred_element_type=F32)

    csend[0] = part(ocore, oxl).astype(BF)
    pl.semaphore_wait(bar, 31 + NZ - 1)
    c0 = remote(csend.at[0], crecv.at[0], s_c.at[0], r_c.at[0], a_core, b)
    c0.start()
    csend[1] = part(ocore, xl).astype(BF)
    c1 = remote(csend.at[1], crecv.at[1], s_c.at[1], r_c.at[1], a_core, b)
    c1.start()
    half_rows = pl.ds(pl.multiple_of(xl * KC, KC), KC)
    e_core = remote(em.at[half_rows, :], em4.at[1], s_e.at[0], r_e.at[0], a_core, b)
    e_core.start()
    e_own = pltpu.make_async_copy(em.at[half_rows, :], em4.at[0], l_e)
    e_own.start()
    own[0] = part(core, oxl)
    own[1] = part(core, xl)
    c0.wait_recv()

    def x_step(i, c):
        zc = zmod(z + 8 + i)
        rows = pl.ds(pl.multiple_of(zc * CH, CH), CH)
        xsend[zc] = (own[0, rows, :] + crecv[0, rows, :].astype(F32)).astype(BF)
        remote(xsend.at[zc], xrecv.at[zc], s_x.at[zc], r_x.at[zc], a_x, b).start()
        return c

    def order(i):
        m = 8 - (i + 1) // 2
        return jnp.where(lax.rem(i, 2) == 0, -m, m)

    def x_ord(i, c):
        return x_step(order(i) - 8, c)

    lax.fori_loop(0, NZ, x_ord, 0)
    c1.wait_recv()

    def z_step(i, c):
        zc = zmod(z + order(i))
        d = zmod(order(i))
        rows = pl.ds(pl.multiple_of(zc * CH, CH), CH)
        remote(xsend.at[zc], xrecv.at[zc], s_x.at[zc], r_x.at[zc], a_x, b).wait_recv()
        total = own[1, rows, :] + crecv[1, rows, :].astype(F32) + xrecv[zc].astype(F32)
        zsend[zc] = total.astype(BF)
        remote(zsend.at[zc], zrecv.at[d], s_z.at[d], r_z.at[d], z_dev(zc), b).start()
        return c

    lax.fori_loop(0, NZ - 1, z_step, 0)
    my_rows = pl.ds(pl.multiple_of(z * CH, CH), CH)
    remote(xsend.at[z], xrecv.at[z], s_x.at[z], r_x.at[z], a_x, b).wait_recv()
    own[0, pl.ds(0, CH), :] = own[1, my_rows, :] + crecv[1, my_rows, :].astype(F32) + xrecv[z].astype(F32)

    other_rows = pl.ds(pl.multiple_of(oxl * KC, KC), KC)
    e_x = remote(em.at[other_rows, :], em4.at[2], s_e.at[1], r_e.at[1], a_x, b)
    e_x.start()

    iota_s = lax.broadcasted_iota(jnp.int32, (HALF, HALF), 0)
    iota_l = lax.broadcasted_iota(jnp.int32, (HALF, HALF), 1)
    te_b = tedge[...].astype(F32).astype(BF)
    for which in range(2):
        h = core if which == 0 else ocore
        lanes = pl.ds(pl.multiple_of(h * HALF, HALF), HALF)
        hot_t = jnp.where(iota_s == dfa[:, lanes], 1.0, 0.0).astype(F32)
        hot = jnp.transpose(hot_t).astype(BF)
        te_h = jnp.dot(hot, te_b, preferred_element_type=F32)
        al = allow[:, lanes].astype(F32)
        al_pad = jnp.concatenate([al, jnp.zeros((126, HALF), F32)], axis=0)
        al_t = jnp.transpose(al_pad)
        ok = jnp.where(iota_l < 128, al_t[:, 0:1], al_t[:, 1:2])
        te_own[h] = jnp.where(ok > 0.0, te_h, 8.0).astype(BF)
        if which == 0:
            suc_t = jnp.dot(edge[...].astype(F32).astype(BF), hot_t.astype(BF), preferred_element_type=F32)
            suc_pad = jnp.concatenate([suc_t, jnp.zeros((120, HALF), F32)], axis=0)
            suc = jnp.transpose(suc_pad).astype(jnp.int32)
    te4[0] = te_own[core]
    t_core = remote(te_own.at[ocore], te4.at[1], s_t.at[0], r_t.at[0], a_core, b)
    t_x = remote(te_own.at[core], te4.at[2], s_t.at[1], r_t.at[1], a_x, b)
    t_d = remote(te_own.at[ocore], te4.at[3], s_t.at[2], r_t.at[2], a_d, b)
    t_core.start()
    t_x.start()
    t_d.start()
    half_cols = pl.ds(pl.multiple_of(xl * KC, KC), KC)
    for k in range(8):
        hot2 = jnp.where(iota_l == suc[:, k : k + 1], 1.0, 0.0).astype(F32).astype(BF)
        g = jnp.dot(hot2, adv[:, half_cols], preferred_element_type=F32).astype(BF)
        gath[k] = g.reshape(NZ, CH, KC)

    def z_add(i, c):
        d = zmod(order(i))
        remote(zsend.at[0], zrecv.at[d], s_z.at[d], r_z.at[d], z_dev(z), b).wait_recv()
        own[0, pl.ds(0, CH), :] += zrecv[d].astype(F32)
        return c

    lax.fori_loop(0, NZ - 1, z_add, 0)
    pri[z] = own[0, pl.ds(0, CH), :].astype(BF)

    def ag_step(i, c):
        d = zmod(order(i))
        remote(pri.at[z], pri.at[z], s_g.at[d], r_g.at[d], z_dev(zmod(z + d)), b).start()
        return c

    lax.fori_loop(0, NZ - 1, ag_step, 0)

    e_x.wait_recv()
    e_f = remote(em4.at[2], em4.at[3], s_e.at[2], r_e.at[2], a_core, b)
    e_f.start()
    e_own.wait()
    e_core.wait_recv()
    t_core.wait_recv()
    t_x.wait_recv()
    t_d.wait_recv()
    e_f.wait_recv()

    lane = lax.broadcasted_iota(jnp.int32, (2 * CH, 128), 1)
    src = xl * 8 + b

    def hid_copy(zc, j):
        qa = [q, 2 * xl + ocore, 2 * oxl + core, 2 * oxl + ocore][j]
        dst = hrecv.at[src, pl.ds(pl.multiple_of(lax.rem(zc, 4) * CH, CH), CH), :]
        return remote(hsend.at[zc, j], dst, s_h.at[zc, j], r_h.at[src], 4 * z + qa, 4 * core + zc // 4)

    def hid_local(zc):
        dst = hrecv.at[src, pl.ds(pl.multiple_of(lax.rem(zc, 4) * CH, CH), CH), :]
        return pltpu.make_async_copy(hsend.at[zc, 0], dst, r_h.at[src])

    def score(t, c):
        zc0 = zmod(z - t)
        zc1 = zmod(z + t + 1)

        @pl.when(t > 0)
        def _():
            remote(pri.at[z], pri.at[zc0], s_g.at[t], r_g.at[t], z_dev(z), b).wait_recv()

        d1 = NZ - 1 - t
        remote(pri.at[z], pri.at[zc1], s_g.at[d1], r_g.at[d1], z_dev(z), b).wait_recv()
        x0 = pri[zc0]
        x1 = pri[zc1]
        for k in range(8):
            wbuf[pl.ds(k * 2 * CH, CH), :] = gath[k, zc0] * x0
            wbuf[pl.ds(k * 2 * CH + CH, CH), :] = gath[k, zc1] * x1
        tot = jnp.zeros((2 * CH, 1), F32)
        for j in range(4):
            cand[...] = jnp.dot(wbuf[...], em4[j], preferred_element_type=F32)
            te = jnp.concatenate(
                [
                    te4[j, pl.ds(pl.multiple_of(zc0 * CH, CH), CH), :],
                    te4[j, pl.ds(pl.multiple_of(zc1 * CH, CH), CH), :],
                ],
                axis=0,
            ).astype(F32)
            chosen = jnp.zeros((2 * CH, TK), F32)
            for k in range(8):
                chosen = jnp.where(te == float(k), cand[pl.ds(k * 2 * CH, 2 * CH), :], chosen)
            tot = tot + jnp.sum(chosen, axis=1, keepdims=True)
            picked = chosen.astype(BF)
            hsend[zc0, j, :, pl.ds(0, TK)] = picked[:CH]
            hsend[zc1, j, :, pl.ds(0, TK)] = picked[CH:]
        hi = tot.astype(BF).astype(F32)
        lo = tot - hi
        tile = jnp.where(lane == 0, hi, jnp.where(lane == 1, lo, 0.0)).astype(BF)
        for j in range(4):
            hsend[zc0, j, :, pl.ds(TK, 128)] = tile[:CH]
            hsend[zc1, j, :, pl.ds(TK, 128)] = tile[CH:]
        for zc in (zc0, zc1):
            for j in (3, 2, 1):
                hid_copy(zc, j).start()
            mine = 4 * core + zc // 4 == b

            @pl.when(mine)
            def _():
                hid_local(zc).start()

            @pl.when(jnp.logical_not(mine))
            def _():
                hid_copy(zc, 0).start()

        return c

    lax.fori_loop(0, NZ // 2, score, 0)

    def h_wait(i, c):
        remote(hrecv.at[i], hrecv.at[i], s_h.at[0, 0], r_h.at[i], a_core, b).wait_recv()
        return c

    lax.fori_loop(0, 16, h_wait, 0)
    acc = jnp.zeros((64, MW), F32)
    for i in range(16):
        acc = acc + hrecv[i].astype(F32)
    scores = acc[:, :TK]
    quad_tot = jnp.sum(acc[:, TK:], axis=1, keepdims=True)
    spread = jnp.concatenate([jnp.broadcast_to(quad_tot, (64, 128)), jnp.zeros((64, 128), F32)], axis=0)
    tsend[...] = jnp.transpose(spread)[0:1]

    def t_step(i, c):
        d = zmod(order(i))
        remote(tsend, trecv.at[d], s_s.at[d], r_s.at[d], z_dev(zmod(z + d)), b).start()
        return c

    lax.fori_loop(0, NZ - 1, t_step, 0)
    mask = te_own[b // 4, pl.ds(pl.multiple_of(lax.rem(b, 4) * 64, 64), 64), :].astype(F32) < 7.5
    logs = jnp.log(jnp.where(mask, scores, 1.0))
    trecv[0] = tsend[...]

    def t_wait(i, c):
        d = zmod(order(i))
        remote(tsend, trecv.at[d], s_s.at[d], r_s.at[d], z_dev(z), b).wait_recv()
        return c

    lax.fori_loop(0, NZ - 1, t_wait, 0)
    full = jnp.zeros((1, 128), F32)
    for d in range(NZ):
        full = full + trecv[d]
    column = jnp.transpose(jnp.broadcast_to(full, (128, 128)))[:64, 0:1]
    out[...] = jnp.where(mask, logs - jnp.log(column), 0.0)

    c0.wait_send()
    c1.wait_send()
    for cp in (e_core, e_x, e_f, t_core, t_x, t_d):
        cp.wait_send()

    def drain(i, c):
        remote(xsend.at[i], xrecv.at[i], s_x.at[i], r_x.at[i], a_x, b).wait_send()
        for j in (1, 2, 3):
            hid_copy(i, j).wait_send()

        @pl.when(4 * core + i // 4 != b)
        def _():
            hid_copy(i, 0).wait_send()

        @pl.when(i > 0)
        def _():
            remote(zsend.at[0], zrecv.at[i], s_z.at[i], r_z.at[i], z_dev(z), b).wait_send()
            remote(pri.at[z], pri.at[z], s_g.at[i], r_g.at[i], z_dev(z), b).wait_send()
            remote(tsend, trecv.at[i], s_s.at[i], r_s.at[i], z_dev(z), b).wait_send()

        return c

    lax.fori_loop(0, NZ, drain, 0)


def body(posterior, transition, emission, advance, dfa_state, edge_next, token_edge, allowed):
    vm = pl.BlockSpec(memory_space=pltpu.VMEM)
    dma = pltpu.SemaphoreType.DMA
    return pl.pallas_call(
        kernel,
        out_shape=jax.ShapeDtypeStruct((64, TK), F32),
        in_specs=[vm] * 8,
        out_specs=vm,
        scratch_shapes=[
            pltpu.VMEM((2, HALF, KC), BF),
            pltpu.VMEM((2, HALF, KC), BF),
            pltpu.VMEM((2, HALF, KC), F32),
            pltpu.VMEM((NZ, CH, KC), BF),
            pltpu.VMEM((NZ, CH, KC), BF),
            pltpu.VMEM((NZ, CH, KC), BF),
            pltpu.VMEM((NZ, CH, KC), BF),
            pltpu.VMEM((NZ, CH, KC), BF),
            pltpu.VMEM((4, KC, TK), BF),
            pltpu.VMEM((2, HALF, TK), BF),
            pltpu.VMEM((4, HALF, TK), BF),
            pltpu.VMEM((8, NZ, CH, KC), BF),
            pltpu.VMEM((HALF, KC), BF),
            pltpu.VMEM((HALF, TK), F32),
            pltpu.VMEM((NZ, 4, CH, MW), BF),
            pltpu.VMEM((16, 64, MW), BF),
            pltpu.VMEM((1, 128), F32),
            pltpu.VMEM((NZ, 1, 128), F32),
            dma((2,)),
            dma((2,)),
            dma((NZ,)),
            dma((NZ,)),
            dma((NZ,)),
            dma((NZ,)),
            dma((NZ,)),
            dma((NZ,)),
            dma((3,)),
            dma((3,)),
            dma((3,)),
            dma((3,)),
            dma((NZ, 4)),
            dma((16,)),
            dma((NZ,)),
            dma((NZ,)),
            dma,
        ],
        compiler_params=pltpu.CompilerParams(
            collective_id=0, has_side_effects=True, vmem_limit_bytes=48 * 1024 * 1024
        ),
        name="constrained",
    )(
        posterior,
        transition,
        emission,
        advance,
        dfa_state.reshape(1, 512),
        edge_next.T,
        token_edge,
        allowed.T,
    )


def solution(mesh):
    in_specs = (
        P(None, "vocab"),
        P("vocab", "hid"),
        P("hid", "vocab"),
        P(None, "hid"),
        P(),
        P(),
        P(None, "vocab"),
        P(None, "vocab"),
    )
    out_specs = P("hid", "vocab")
    return jax.shard_map(body, mesh=mesh, in_specs=in_specs, out_specs=out_specs, check_vma=False)
```

```python
import jax
import jax.numpy as jnp
from jax import lax
from jax.experimental import pallas as pl
from jax.experimental.pallas import tpu as pltpu
from jax.sharding import PartitionSpec as P

MESH = pl.DeviceIdType.MESH
BF = jnp.bfloat16
F32 = jnp.float32
NZ = 16
CH = 16
HALF = 256
KC = 1024
TK = 256
MW = 384
TARGET = {
    -3: 2, -4: 1, -6: -1, -7: -2, 8: -3, 3: -2, 4: -1, 6: 1, 7: 2,
    1: 1, -1: -1, 2: 2, -2: -2, 5: 5, -5: -5,
}
FIRST = (8, -3, 3, -7, 7, -4, 4, -6, 6)
X_ORDER = FIRST + (-5, 5, -2, 2, -1, 1, 0)
BARRIER_STEPS = (5, -5, 3, -3, 2, -2, 1, -1)


def remote(src, dst, send, recv, a, b):
    return pltpu.make_async_remote_copy(
        src_ref=src,
        dst_ref=dst,
        send_sem=send,
        recv_sem=recv,
        device_id={"vocab": a, "hid": b},
        device_id_type=MESH,
    )


def kernel(
    post_h,
    trans_h,
    em_h,
    adv_h,
    dfa_h,
    edge_h,
    tedge_h,
    allow_h,
    out,
    post,
    trans,
    adv,
    dfa,
    edge,
    tedge,
    allow,
    csend,
    crecv,
    own,
    xsend,
    xrecv,
    zsend,
    zrecv,
    agg,
    pri,
    em4,
    tab4,
    te4,
    gath,
    wbuf,
    cand,
    hsend,
    hrecv,
    tsend,
    trecv,
    allowed_rows,
    l_in,
    s_c,
    r_c,
    s_x,
    r_x,
    s_z,
    r_z,
    s_g,
    r_g,
    s_e,
    r_e,
    s_t,
    r_t,
    s_h,
    r_h,
    s_s,
    r_s,
):
    a = lax.axis_index("vocab")
    b = lax.axis_index("hid")
    z = a // 4
    q = lax.rem(a, 4)
    xl = q // 2
    core = lax.rem(q, 2)
    ocore = 1 - core
    oxl = 1 - xl
    a_core = 4 * z + 2 * xl + ocore
    a_x = 4 * z + 2 * oxl + core

    half_rows = pl.ds(pl.multiple_of(xl * KC, KC), KC)
    other_rows = pl.ds(pl.multiple_of(oxl * KC, KC), KC)
    loads = [
        pltpu.make_async_copy(post_h, post, l_in.at[0]),
        pltpu.make_async_copy(trans_h, trans, l_in.at[1]),
        pltpu.make_async_copy(tedge_h, tedge, l_in.at[2]),
        pltpu.make_async_copy(allow_h, allow, l_in.at[3]),
        pltpu.make_async_copy(dfa_h, dfa, l_in.at[4]),
        pltpu.make_async_copy(edge_h, edge, l_in.at[5]),
        pltpu.make_async_copy(adv_h.at[:, half_rows], adv, l_in.at[6]),
        pltpu.make_async_copy(em_h.at[half_rows, :], em4.at[0], l_in.at[7]),
    ]
    for cp in loads:
        cp.start()

    def zmod(v):
        return lax.rem(v + 2 * NZ, NZ)

    def z_dev(step):
        return 4 * zmod(z + step) + q

    bar = pltpu.get_barrier_semaphore()

    def sig_group(i, c):
        m = lax.rem(q * 8 + b + i, 32)
        pl.semaphore_signal(
            bar, inc=1, device_id={"vocab": 4 * z + m // 8, "hid": lax.rem(m, 8)}, device_id_type=MESH
        )
        return c

    for step in BARRIER_STEPS:
        pl.semaphore_signal(bar, inc=1, device_id={"vocab": z_dev(step), "hid": b}, device_id_type=MESH)
    lax.fori_loop(1, 32, sig_group, 0)

    def part(row_half, col_half):
        rows = pl.ds(pl.multiple_of(row_half * HALF, HALF), HALF)
        cols = pl.ds(pl.multiple_of(col_half * KC, KC), KC)
        return jnp.dot(post[rows, :], trans[:, cols], preferred_element_type=F32)

    loads[0].wait()
    loads[1].wait()
    csend[0] = part(ocore, oxl).astype(BF)
    pl.semaphore_wait(bar, 31 + len(BARRIER_STEPS))
    c0 = remote(csend.at[0], crecv.at[0], s_c.at[0], r_c.at[0], a_core, b)
    c0.start()
    csend[1] = part(ocore, xl).astype(BF)
    c1 = remote(csend.at[1], crecv.at[1], s_c.at[1], r_c.at[1], a_core, b)
    c1.start()

    loads[2].wait()
    loads[3].wait()
    tab4[0, pl.ds(0, HALF), :] = tedge[...].astype(F32).astype(BF)
    al = allow[...].astype(F32)
    al_rows = jnp.concatenate([al[:, :HALF], al[:, HALF:], jnp.zeros((12, HALF), F32)], axis=0)
    tab4[0, pl.ds(HALF, 16), :] = al_rows.astype(BF)
    t_core = remote(tab4.at[0], tab4.at[1], s_t.at[0], r_t.at[0], a_core, b)
    t_x = remote(tab4.at[0], tab4.at[2], s_t.at[1], r_t.at[1], a_x, b)
    t_core.start()
    t_x.start()

    own[0] = part(core, oxl)
    own[1] = part(core, xl)
    c0.wait_recv()

    def x_copy(zc):
        return remote(xsend.at[zc], xrecv.at[zc], s_x.at[zc], r_x.at[zc], a_x, b)

    for o in X_ORDER:
        zc = zmod(z + o)
        rows = pl.ds(pl.multiple_of(zc * CH, CH), CH)
        xsend[zc] = (own[0, rows, :] + crecv[0, rows, :].astype(F32)).astype(BF)
        x_copy(zc).start()
    e_core = remote(em_h.at[half_rows, :], em4.at[1], s_e.at[0], r_e.at[0], a_core, b)
    e_core.start()
    c1.wait_recv()

    def reduced(o):
        zc = zmod(z + o)
        rows = pl.ds(pl.multiple_of(zc * CH, CH), CH)
        x_copy(zc).wait_recv()
        return own[1, rows, :] + crecv[1, rows, :].astype(F32) + xrecv[zc].astype(F32)

    def z_copy(o):
        i = o % NZ
        return remote(zsend.at[i], zrecv.at[i], s_z.at[i], r_z.at[i], z_dev(TARGET[o]), b)

    def z_send(o, value):
        zsend[o % NZ] = value.astype(BF)
        z_copy(o).start()

    def z_take(o):
        z_copy(o).wait_recv()
        return zrecv[o % NZ].astype(F32)

    for o in FIRST:
        z_send(o, reduced(o))
    agg[0] = reduced(-5)
    agg[1] = reduced(5)
    for o in (-2, 2):
        z_send(o, reduced(o))
    total = agg[0]
    for o in (-3, -4, -6, -7, 8):
        total = total + z_take(o)
    z_send(-5, total)
    total = agg[1]
    for o in (3, 4, 6, 7):
        total = total + z_take(o)
    z_send(5, total)
    for o in (-1, 1):
        z_send(o, reduced(o))
    agg[0] = reduced(0)

    e_x = remote(em_h.at[other_rows, :], em4.at[2], s_e.at[1], r_e.at[1], a_x, b)
    e_x.start()
    t_x.wait_recv()
    t_f = remote(tab4.at[2], tab4.at[3], s_t.at[2], r_t.at[2], a_core, b)
    t_f.start()

    for i in (4, 5, 6):
        loads[i].wait()
    iota_s = lax.broadcasted_iota(jnp.int32, (HALF, HALF), 0)
    iota_l = lax.broadcasted_iota(jnp.int32, (HALF, HALF), 1)
    lanes = pl.ds(pl.multiple_of(core * HALF, HALF), HALF)
    hot_t = jnp.where(iota_s == dfa[:, lanes], 1.0, 0.0).astype(F32)
    suc_t = jnp.dot(edge[...].astype(F32).astype(BF), hot_t.astype(BF), preferred_element_type=F32)
    suc = jnp.transpose(jnp.concatenate([suc_t, jnp.zeros((120, HALF), F32)], axis=0)).astype(jnp.int32)
    for k in range(8):
        hot2 = jnp.where(iota_l == suc[:, k : k + 1], 1.0, 0.0).astype(F32).astype(BF)
        g = jnp.dot(hot2, adv[...], preferred_element_type=F32).astype(BF)
        gath[k] = g.reshape(NZ, CH, KC)

    total = agg[0]
    for o in (-1, 1, -2, 2, -5, 5):
        total = total + z_take(o)
    pri[z] = total.astype(BF)

    def g_copy(chunk, step, o):
        zc = zmod(z + chunk)
        i = o % NZ
        return remote(pri.at[zc], pri.at[zc], s_g.at[i], r_g.at[i], z_dev(step), b)

    for step in (5, -5, 1, -1, 2, -2):
        g_copy(0, step, -step).start()

    hot = jnp.transpose(hot_t).astype(BF)
    t_core.wait_recv()
    t_f.wait_recv()
    for j in range(4):
        te = jnp.dot(hot, tab4[j, pl.ds(0, HALF), :], preferred_element_type=F32)
        al = tab4[j, pl.ds(HALF, 16), :].astype(F32)
        al = jnp.where(core == 0, al[0:2], al[2:4])
        al_t = jnp.transpose(jnp.concatenate([al, jnp.zeros((126, HALF), F32)], axis=0))
        ok = jnp.where(iota_l < 128, al_t[:, 0:1], al_t[:, 1:2])
        te4[j] = jnp.where(ok > 0.0, te, 8.0).astype(BF)

    lane = lax.broadcasted_iota(jnp.int32, (2 * CH, 128), 1)
    src = xl * 8 + b

    def hid_copy(zc, j):
        qa = [q, 2 * xl + ocore, 2 * oxl + core, 2 * oxl + ocore][j]
        dst = hrecv.at[src, pl.ds(pl.multiple_of(lax.rem(zc, 4) * CH, CH), CH), :]
        return remote(hsend.at[zc, j], dst, s_h.at[zc, j], r_h.at[src], 4 * z + qa, 4 * core + zc // 4)

    def hid_local(zc):
        dst = hrecv.at[src, pl.ds(pl.multiple_of(lax.rem(zc, 4) * CH, CH), CH), :]
        return pltpu.make_async_copy(hsend.at[zc, 0], dst, r_h.at[src])

    def pri_wait(o):
        i = zmod(o)
        zc = zmod(z + o)
        remote(pri.at[z], pri.at[zc], s_g.at[i], r_g.at[i], z_dev(1), b).wait_recv()

    def score(t, c):
        m = jnp.where(t < 2, t + 1, jnp.where(t == 2, 5, jnp.where(t == 3, 4, jnp.where(t == 4, 3, t + 1))))
        o0 = jnp.where(t == 7, 0, -m)
        zc0 = zmod(z + o0)
        zc1 = zmod(z + m)

        @pl.when(jnp.logical_and(t != 7, t != 2))
        def _():
            pri_wait(o0)

        @pl.when(t != 2)
        def _():
            pri_wait(m)

        x0 = pri[zc0]
        x1 = pri[zc1]
        for k in range(8):
            wbuf[pl.ds(k * 2 * CH, CH), :] = gath[k, zc0] * x0
            wbuf[pl.ds(k * 2 * CH + CH, CH), :] = gath[k, zc1] * x1
        for j in range(4):
            cand[j] = jnp.dot(wbuf[...], em4[j], preferred_element_type=F32)
        tot = jnp.zeros((2 * CH, 1), F32)
        for j in range(4):
            te = jnp.concatenate(
                [
                    te4[j, pl.ds(pl.multiple_of(zc0 * CH, CH), CH), :],
                    te4[j, pl.ds(pl.multiple_of(zc1 * CH, CH), CH), :],
                ],
                axis=0,
            ).astype(F32)
            chosen = jnp.zeros((2 * CH, TK), F32)
            for k in range(8):
                chosen = jnp.where(te == float(k), cand[j, pl.ds(k * 2 * CH, 2 * CH), :], chosen)
            tot = tot + jnp.sum(chosen, axis=1, keepdims=True)
            picked = chosen.astype(BF)
            hsend[zc0, j, :, pl.ds(0, TK)] = picked[:CH]
            hsend[zc1, j, :, pl.ds(0, TK)] = picked[CH:]
        hi = tot.astype(BF).astype(F32)
        lo = tot - hi
        tile = jnp.where(lane == 0, hi, jnp.where(lane == 1, lo, 0.0)).astype(BF)
        for j in range(4):
            hsend[zc0, j, :, pl.ds(TK, 128)] = tile[:CH]
            hsend[zc1, j, :, pl.ds(TK, 128)] = tile[CH:]
        for zc in (zc0, zc1):
            for j in (3, 2, 1):
                hid_copy(zc, j).start()
            mine = 4 * core + zc // 4 == b

            @pl.when(mine)
            def _():
                hid_local(zc).start()

            @pl.when(jnp.logical_not(mine))
            def _():
                hid_copy(zc, 0).start()

        @pl.when(t == 1)
        def _():
            pri_wait(-5)
            for step in (3, -2, 2, -1, 1):
                g_copy(-5, step, -5 - step).start()
            pri_wait(5)
            for step in (2, -2, 1, -1):
                g_copy(5, step, 5 - step).start()

        return c

    loads[7].wait()
    e_core.wait_recv()
    e_x.wait_recv()
    e_f = remote(em4.at[2], em4.at[3], s_e.at[2], r_e.at[2], a_core, b)
    e_f.start()
    e_f.wait_recv()
    lax.fori_loop(0, NZ // 2, score, 0)

    def h_wait(i, c):
        remote(hrecv.at[i], hrecv.at[i], s_h.at[0, 0], r_h.at[i], a_core, b).wait_recv()
        return c

    lax.fori_loop(0, 16, h_wait, 0)
    acc = jnp.zeros((64, MW), F32)
    for i in range(16):
        acc = acc + hrecv[i].astype(F32)
    scores = acc[:, :TK]
    quad_tot = jnp.sum(acc[:, TK:], axis=1, keepdims=True)
    spread = jnp.concatenate([jnp.broadcast_to(quad_tot, (64, 128)), jnp.zeros((64, 128), F32)], axis=0)
    tsend[...] = jnp.transpose(spread)[0:1]

    def t_copy(i):
        d = zmod(i)
        return remote(tsend, trecv.at[d], s_s.at[d], r_s.at[d], z_dev(i), b)

    def t_step(i, c):
        t_copy(lax.rem(i + 7, 15) + 1).start()
        return c

    lax.fori_loop(0, NZ - 1, t_step, 0)
    al = tab4[0, pl.ds(HALF, 16), :].astype(F32)
    al = jnp.where(b < 4, al[0:2], al[2:4])
    al_t = jnp.transpose(jnp.concatenate([al, jnp.zeros((126, HALF), F32)], axis=0))
    allowed_rows[...] = al_t
    al_t = allowed_rows[pl.ds(pl.multiple_of(lax.rem(b, 4) * 64, 64), 64), :]
    lane_v = lax.broadcasted_iota(jnp.int32, (64, TK), 1)
    mask = jnp.where(lane_v < 128, al_t[:, 0:1], al_t[:, 1:2]) > 0.0
    logs = jnp.log(jnp.where(mask, scores, 1.0))
    trecv[0] = tsend[...]

    def t_wait(i, c):
        t_copy(i).wait_recv()
        return c

    lax.fori_loop(1, NZ, t_wait, 0)
    full = jnp.zeros((1, 128), F32)
    for d in range(NZ):
        full = full + trecv[d]
    column = jnp.transpose(jnp.broadcast_to(full, (128, 128)))[:64, 0:1]
    out[...] = jnp.where(mask, logs - jnp.log(column), 0.0)

    for cp in (c0, c1, e_core, e_x, e_f, t_core, t_x, t_f):
        cp.wait_send()

    def drain(i, c):
        x_copy(i).wait_send()
        for j in (1, 2, 3):
            hid_copy(i, j).wait_send()

        @pl.when(4 * core + i // 4 != b)
        def _():
            hid_copy(i, 0).wait_send()

        @pl.when(i > 0)
        def _():
            remote(zsend.at[i], zrecv.at[i], s_z.at[i], r_z.at[i], z_dev(1), b).wait_send()
            remote(pri.at[z], pri.at[z], s_g.at[i], r_g.at[i], z_dev(1), b).wait_send()
            t_copy(i).wait_send()

        return c

    lax.fori_loop(0, NZ, drain, 0)


def body(posterior, transition, emission, advance, dfa_state, edge_next, token_edge, allowed):
    vm = pl.BlockSpec(memory_space=pltpu.VMEM)
    dma = pltpu.SemaphoreType.DMA
    return pl.pallas_call(
        kernel,
        out_shape=jax.ShapeDtypeStruct((64, TK), F32),
        in_specs=[pl.BlockSpec(memory_space=pltpu.HBM)] * 8,
        out_specs=vm,
        scratch_shapes=[
            pltpu.VMEM((512, 256), BF),
            pltpu.VMEM((256, 2 * KC), BF),
            pltpu.VMEM((256, KC), BF),
            pltpu.VMEM((1, 512), jnp.int32),
            pltpu.VMEM((8, 256), jnp.int32),
            pltpu.VMEM((256, TK), jnp.int32),
            pltpu.VMEM((2, 512), jnp.int32),
            pltpu.VMEM((2, HALF, KC), BF),
            pltpu.VMEM((2, HALF, KC), BF),
            pltpu.VMEM((2, HALF, KC), F32),
            pltpu.VMEM((NZ, CH, KC), BF),
            pltpu.VMEM((NZ, CH, KC), BF),
            pltpu.VMEM((NZ, CH, KC), BF),
            pltpu.VMEM((NZ, CH, KC), BF),
            pltpu.VMEM((2, CH, KC), F32),
            pltpu.VMEM((NZ, CH, KC), BF),
            pltpu.VMEM((4, KC, TK), BF),
            pltpu.VMEM((4, HALF + 16, TK), BF),
            pltpu.VMEM((4, HALF, TK), BF),
            pltpu.VMEM((8, NZ, CH, KC), BF),
            pltpu.VMEM((HALF, KC), BF),
            pltpu.VMEM((4, HALF, TK), F32),
            pltpu.VMEM((NZ, 4, CH, MW), BF),
            pltpu.VMEM((16, 64, MW), BF),
            pltpu.VMEM((1, 128), F32),
            pltpu.VMEM((NZ, 1, 128), F32),
            pltpu.VMEM((HALF, 128), F32),
            dma((8,)),
            dma((2,)),
            dma((2,)),
            dma((NZ,)),
            dma((NZ,)),
            dma((NZ,)),
            dma((NZ,)),
            dma((NZ,)),
            dma((NZ,)),
            dma((3,)),
            dma((3,)),
            dma((3,)),
            dma((3,)),
            dma((NZ, 4)),
            dma((16,)),
            dma((NZ,)),
            dma((NZ,)),
        ],
        compiler_params=pltpu.CompilerParams(
            collective_id=0, has_side_effects=True, vmem_limit_bytes=62 * 1024 * 1024
        ),
        name="constrained",
    )(
        posterior,
        transition,
        emission,
        advance,
        dfa_state.reshape(1, 512),
        edge_next.T,
        token_edge,
        allowed.T,
    )


def solution(mesh):
    in_specs = (
        P(None, "vocab"),
        P("vocab", "hid"),
        P("hid", "vocab"),
        P(None, "hid"),
        P(),
        P(),
        P(None, "vocab"),
        P(None, "vocab"),
    )
    out_specs = P("hid", "vocab")
    return jax.shard_map(body, mesh=mesh, in_specs=in_specs, out_specs=out_specs, check_vma=False)
```

```python
import jax
import jax.numpy as jnp
from jax import lax
from jax.experimental import pallas as pl
from jax.experimental.pallas import tpu as pltpu
from jax.sharding import PartitionSpec as P

MESH = pl.DeviceIdType.MESH
BF = jnp.bfloat16
F32 = jnp.float32
NZ = 16
CH = 16
HALF = 256
KC = 1024
TK = 256
TARGET = {
    -4: 1, -6: -1, -7: -2, 8: -3, 4: -1, 6: 1, 7: 2,
    1: 1, -1: -1, 2: 2, -2: -2, 3: 3, -3: -3, 5: 5, -5: -5,
}
FIRST = (8, -7, 7, -4, 4, -6, 6)
X_ORDER = FIRST + (-5, 5, -3, 3, -2, 2, -1, 1, 0)
BARRIER_STEPS = (3, -3, 2, -2, 1, -1)
EB = 4
ER = KC // EB


def remote(src, dst, send, recv, a, b):
    return pltpu.make_async_remote_copy(
        src_ref=src,
        dst_ref=dst,
        send_sem=send,
        recv_sem=recv,
        device_id={"vocab": a, "hid": b},
        device_id_type=MESH,
    )


def kernel(
    post_h,
    trans_h,
    em_h,
    adv_h,
    dfa_h,
    edge_h,
    tedge_h,
    allow_h,
    out,
    post,
    trans,
    adv,
    dfa,
    edge,
    tedge,
    allow,
    csend,
    crecv,
    own,
    xsend,
    xrecv,
    zsend,
    zrecv,
    agg,
    pri,
    em4,
    tab4,
    te4,
    gath,
    wbuf,
    cand,
    hsend,
    hrecv,
    tsend,
    trecv,
    usend,
    urecv,
    tcol,
    logs,
    allowed_rows,
    suc,
    hot,
    l_in,
    s_c,
    r_c,
    s_x,
    r_x,
    s_z,
    r_z,
    s_g,
    r_g,
    s_e,
    r_e,
    s_t,
    r_t,
    s_h,
    r_h,
    s_s,
    r_s,
    s_u,
    r_u,
):
    a = lax.axis_index("vocab")
    b = lax.axis_index("hid")
    z = a // 4
    q = lax.rem(a, 4)
    xl = q // 2
    core = lax.rem(q, 2)
    ocore = 1 - core
    oxl = 1 - xl
    a_core = 4 * z + 2 * xl + ocore
    a_x = 4 * z + 2 * oxl + core

    half_rows = pl.ds(pl.multiple_of(xl * KC, KC), KC)
    loads = [
        pltpu.make_async_copy(post_h, post, l_in.at[0]),
        pltpu.make_async_copy(trans_h, trans, l_in.at[1]),
        pltpu.make_async_copy(tedge_h, tedge, l_in.at[2]),
        pltpu.make_async_copy(allow_h, allow, l_in.at[3]),
        pltpu.make_async_copy(dfa_h, dfa, l_in.at[4]),
        pltpu.make_async_copy(edge_h, edge, l_in.at[5]),
        pltpu.make_async_copy(adv_h.at[:, half_rows], adv, l_in.at[6]),
        pltpu.make_async_copy(em_h.at[half_rows, :], em4.at[0], l_in.at[7]),
    ]
    for cp in loads:
        cp.start()

    def zmod(v):
        return lax.rem(v + 2 * NZ, NZ)

    def z_dev(step):
        return 4 * zmod(z + step) + q

    bar = pltpu.get_barrier_semaphore()

    def sig_group(i, c):
        m = lax.rem(q * 8 + b + i, 32)
        pl.semaphore_signal(
            bar, inc=1, device_id={"vocab": 4 * z + m // 8, "hid": lax.rem(m, 8)}, device_id_type=MESH
        )
        return c

    for step in BARRIER_STEPS:
        pl.semaphore_signal(bar, inc=1, device_id={"vocab": z_dev(step), "hid": b}, device_id_type=MESH)
    lax.fori_loop(1, 32, sig_group, 0)

    def part(row_half, col_half):
        rows = pl.ds(pl.multiple_of(row_half * HALF, HALF), HALF)
        cols = pl.ds(pl.multiple_of(col_half * KC, KC), KC)
        return jnp.dot(post[rows, :], trans[:, cols], preferred_element_type=F32)

    loads[0].wait()
    loads[1].wait()
    csend[0] = part(ocore, oxl).astype(BF)
    pl.semaphore_wait(bar, 31 + len(BARRIER_STEPS))
    c0 = remote(csend.at[0], crecv.at[0], s_c.at[0], r_c.at[0], a_core, b)
    c0.start()

    def e_copy(i):
        rows = pl.ds(pl.multiple_of(oxl * KC + i * ER, ER), ER)
        return remote(em_h.at[rows, :], em4.at[2, pl.ds(i * ER, ER), :], s_e.at[1 + i], r_e.at[1 + i], a_x, b)

    def f_copy(i):
        rows = pl.ds(i * ER, ER)
        return remote(em4.at[2, rows, :], em4.at[3, rows, :], s_e.at[5 + i], r_e.at[5 + i], a_core, b)

    e_copy(0).start()
    csend[1] = part(ocore, xl).astype(BF)
    c1 = remote(csend.at[1], crecv.at[1], s_c.at[1], r_c.at[1], a_core, b)
    c1.start()

    loads[2].wait()
    loads[3].wait()
    tab4[0, pl.ds(0, HALF), :] = tedge[...].astype(F32).astype(BF)
    al = allow[...].astype(F32)
    al_rows = jnp.concatenate([al[:, :HALF], al[:, HALF:], jnp.zeros((12, HALF), F32)], axis=0)
    tab4[0, pl.ds(HALF, 16), :] = al_rows.astype(BF)
    t_core = remote(tab4.at[0], tab4.at[1], s_t.at[0], r_t.at[0], a_core, b)
    t_x = remote(tab4.at[0], tab4.at[2], s_t.at[1], r_t.at[1], a_x, b)
    t_core.start()

    own[0] = part(core, oxl)
    c0.wait_recv()

    def x_copy(zc):
        return remote(xsend.at[zc], xrecv.at[zc], s_x.at[zc], r_x.at[zc], a_x, b)

    for o in X_ORDER:
        zc = zmod(z + o)
        rows = pl.ds(pl.multiple_of(zc * CH, CH), CH)
        xsend[zc] = (own[0, rows, :] + crecv[0, rows, :].astype(F32)).astype(BF)
        x_copy(zc).start()
    e_core = remote(em_h.at[half_rows, :], em4.at[1], s_e.at[0], r_e.at[0], a_core, b)
    e_core.start()
    own[1] = part(core, xl)

    for i in (4, 5, 6):
        loads[i].wait()
    iota_s = lax.broadcasted_iota(jnp.int32, (HALF, HALF), 0)
    iota_l = lax.broadcasted_iota(jnp.int32, (HALF, HALF), 1)
    lanes = pl.ds(pl.multiple_of(core * HALF, HALF), HALF)
    hot_t = jnp.where(iota_s == dfa[:, lanes], 1.0, 0.0).astype(F32)
    suc_t = jnp.dot(edge[...].astype(F32).astype(BF), hot_t.astype(BF), preferred_element_type=F32)
    suc[...] = jnp.transpose(jnp.concatenate([suc_t, jnp.zeros((120, HALF), F32)], axis=0)).astype(jnp.int32)
    hot[...] = jnp.transpose(hot_t).astype(BF)

    def gather(k):
        hot2 = jnp.where(iota_l == suc[:, pl.ds(k, 1)], 1.0, 0.0).astype(F32).astype(BF)
        g = jnp.dot(hot2, adv[...], preferred_element_type=F32).astype(BF)
        gath[k] = g.reshape(NZ, CH, KC)

    gather(0)
    gather(1)
    c1.wait_recv()

    def reduced(o):
        zc = zmod(z + o)
        rows = pl.ds(pl.multiple_of(zc * CH, CH), CH)
        x_copy(zc).wait_recv()
        return own[1, rows, :] + crecv[1, rows, :].astype(F32) + xrecv[zc].astype(F32)

    def z_copy(o):
        i = o % NZ
        return remote(zsend.at[i], zrecv.at[i], s_z.at[i], r_z.at[i], z_dev(TARGET[o]), b)

    def z_send(o, value):
        zsend[o % NZ] = value.astype(BF)
        z_copy(o).start()

    def z_take(o):
        z_copy(o).wait_recv()
        return zrecv[o % NZ].astype(F32)

    for k, o in enumerate(FIRST):
        z_send(o, reduced(o))
        if k < 6:
            gather(k + 2)
    low = reduced(-5)
    for o in (8, -7, -4, -6):
        low = low + z_take(o)
    agg[0] = low
    high = reduced(5)
    for o in (7, 4, 6):
        high = high + z_take(o)
    z_send(-5, agg[0])
    z_send(5, high)
    t_x.start()
    for i in range(1, EB):
        e_copy(i).start()
    for o in (-3, 3, -2, 2, -1, 1):
        z_send(o, reduced(o))
    agg[0] = reduced(0)
    e_copy(0).wait_recv()
    f_copy(0).start()
    t_x.wait_recv()
    t_f = remote(tab4.at[2], tab4.at[3], s_t.at[2], r_t.at[2], a_core, b)
    t_f.start()

    total = agg[0]
    for o in (-1, 1, -2, 2, -3, 3, -5, 5):
        total = total + z_take(o)
    pri[z] = total.astype(BF)

    def g_copy(chunk, step, o):
        zc = zmod(z + chunk)
        i = o % NZ
        return remote(pri.at[zc], pri.at[zc], s_g.at[i], r_g.at[i], z_dev(step), b)

    for step in (5, -5):
        g_copy(0, step, -step).start()

    t_core.wait_recv()
    t_f.wait_recv()
    for j in range(4):
        te = jnp.dot(hot[...], tab4[j, pl.ds(0, HALF), :], preferred_element_type=F32)
        al = tab4[j, pl.ds(HALF, 16), :].astype(F32)
        al = jnp.where(core == 0, al[0:2], al[2:4])
        al_t = jnp.transpose(jnp.concatenate([al, jnp.zeros((126, HALF), F32)], axis=0))
        ok = jnp.where(iota_l < 128, al_t[:, 0:1], al_t[:, 1:2])
        te4[j] = jnp.where(ok > 0.0, te, 8.0).astype(BF)
    for step in (3, -3, 2, -2, 1, -1):
        g_copy(0, step, -step).start()

    src = xl * 8 + b

    def hid_copy(zc, j):
        qa = [q, 2 * xl + ocore, 2 * oxl + core, 2 * oxl + ocore][j]
        dst = hrecv.at[src, pl.ds(pl.multiple_of(lax.rem(zc, 4) * CH, CH), CH), :]
        return remote(hsend.at[zc, j], dst, s_h.at[zc, j], r_h.at[src], 4 * z + qa, 4 * core + zc // 4)

    def hid_local(zc):
        dst = hrecv.at[src, pl.ds(pl.multiple_of(lax.rem(zc, 4) * CH, CH), CH), :]
        return pltpu.make_async_copy(hsend.at[zc, 0], dst, r_h.at[src])

    def pri_wait(o):
        i = zmod(o)
        zc = zmod(z + o)
        remote(pri.at[z], pri.at[zc], s_g.at[i], r_g.at[i], z_dev(1), b).wait_recv()

    def score(t, c):
        m = jnp.where(t == 3, 5, jnp.where(t == 4, 4, t + 1))
        o0 = jnp.where(t == 7, 0, -m)
        zc0 = zmod(z + o0)
        zc1 = zmod(z + m)

        @pl.when(jnp.logical_and(t != 7, t != 3))
        def _():
            pri_wait(o0)

        @pl.when(t != 3)
        def _():
            pri_wait(m)

        x0 = pri[zc0]
        x1 = pri[zc1]
        for k in range(8):
            wbuf[pl.ds(k * 2 * CH, CH), :] = gath[k, zc0] * x0
            wbuf[pl.ds(k * 2 * CH + CH, CH), :] = gath[k, zc1] * x1
        for j in range(4):
            cand[j] = jnp.dot(wbuf[...], em4[j], preferred_element_type=F32)
        tot = jnp.zeros((2 * CH, 1), F32)
        for j in range(4):
            te = jnp.concatenate(
                [
                    te4[j, pl.ds(pl.multiple_of(zc0 * CH, CH), CH), :],
                    te4[j, pl.ds(pl.multiple_of(zc1 * CH, CH), CH), :],
                ],
                axis=0,
            ).astype(F32)
            chosen = jnp.zeros((2 * CH, TK), F32)
            for k in range(8):
                chosen = jnp.where(te == float(k), cand[j, pl.ds(k * 2 * CH, 2 * CH), :], chosen)
            tot = tot + jnp.sum(chosen, axis=1, keepdims=True)
            picked = chosen.astype(BF)
            hsend[zc0, j] = picked[:CH]
            hsend[zc1, j] = picked[CH:]
        wide = jnp.broadcast_to(tot, (2 * CH, 128))
        tcol[pl.ds(pl.multiple_of(zc0 * CH, CH), CH), :] = wide[:CH]
        tcol[pl.ds(pl.multiple_of(zc1 * CH, CH), CH), :] = wide[CH:]
        for zc in (zc0, zc1):
            for j in (3, 2, 1):
                hid_copy(zc, j).start()
            mine = 4 * core + zc // 4 == b

            @pl.when(mine)
            def _():
                hid_local(zc).start()

            @pl.when(jnp.logical_not(mine))
            def _():
                hid_copy(zc, 0).start()

        @pl.when(t == 0)
        def _():
            pri_wait(-5)
            for step in (3, 2, -1, 1):
                g_copy(-5, step, -5 - step).start()
            pri_wait(5)
            for step in (-2, 1, -1):
                g_copy(5, step, 5 - step).start()

        return c

    loads[7].wait()
    e_core.wait_recv()
    for i in range(1, EB):
        e_copy(i).wait_recv()
        f_copy(i).start()
    for i in range(EB):
        f_copy(i).wait_recv()
    lax.fori_loop(0, NZ // 2, score, 0)

    tsend[0:1] = jnp.transpose(tcol[pl.ds(0, 128), :])[0:1]
    tsend[1:2] = jnp.transpose(tcol[pl.ds(128, 128), :])[0:1]

    def t_copy(i):
        d = zmod(i)
        return remote(tsend, trecv.at[d], s_s.at[d], r_s.at[d], z_dev(i), b)

    def t_step(i, c):
        t_copy(lax.rem(i + 7, 15) + 1).start()
        return c

    lax.fori_loop(0, NZ - 1, t_step, 0)
    trecv[0] = tsend[...]

    def h_wait(i, c):
        remote(hrecv.at[i], hrecv.at[i], s_h.at[0, 0], r_h.at[i], a_core, b).wait_recv()
        return c

    lax.fori_loop(0, 16, h_wait, 0)
    scores = jnp.zeros((64, TK), F32)
    for i in range(16):
        scores = scores + hrecv[i].astype(F32)
    al = tab4[0, pl.ds(HALF, 16), :].astype(F32)
    al = jnp.where(b < 4, al[0:2], al[2:4])
    al_t = jnp.transpose(jnp.concatenate([al, jnp.zeros((126, HALF), F32)], axis=0))
    allowed_rows[...] = al_t
    al_t = allowed_rows[pl.ds(pl.multiple_of(lax.rem(b, 4) * 64, 64), 64), :]
    lane_v = lax.broadcasted_iota(jnp.int32, (64, TK), 1)
    mask = jnp.where(lane_v < 128, al_t[:, 0:1], al_t[:, 1:2]) > 0.0
    logs[...] = jnp.log(jnp.where(mask, scores, 1.0))

    def t_wait(i, c):
        t_copy(i).wait_recv()
        return c

    lax.fori_loop(1, NZ, t_wait, 0)
    part_tot = trecv[0]
    for d in range(1, NZ):
        part_tot = part_tot + trecv[d]
    usend[0] = part_tot[0:1]
    usend[1] = part_tot[1:2]

    def u_copy(i, j):
        qa = [q, 2 * xl + ocore, 2 * oxl + core, 2 * oxl + ocore][j]
        return remote(usend.at[i // 2], urecv.at[src], s_u.at[i, j], r_u.at[src], 4 * z + qa, 4 * core + i)

    for i in range(4):
        for j in (3, 2, 1):
            u_copy(i, j).start()
        mine = 4 * core + i == b

        @pl.when(mine)
        def _():
            pltpu.make_async_copy(usend.at[i // 2], urecv.at[src], r_u.at[src]).start()

        @pl.when(jnp.logical_not(mine))
        def _():
            u_copy(i, 0).start()

    def u_wait(i, c):
        remote(urecv.at[i], urecv.at[i], s_u.at[0, 0], r_u.at[i], a_core, b).wait_recv()
        return c

    lax.fori_loop(0, 16, u_wait, 0)
    full = urecv[0]
    for i in range(1, 16):
        full = full + urecv[i]
    column = jnp.transpose(jnp.broadcast_to(full, (128, 128)))
    column = jnp.where(lax.rem(b, 2) == 0, column[:64, 0:1], column[64:, 0:1])
    out[...] = jnp.where(mask, logs[...] - jnp.log(column), 0.0)

    for cp in (c0, c1, e_core, t_core, t_x, t_f):
        cp.wait_send()
    for i in range(EB):
        e_copy(i).wait_send()
        f_copy(i).wait_send()

    def drain(i, c):
        x_copy(i).wait_send()
        for j in (1, 2, 3):
            hid_copy(i, j).wait_send()

        @pl.when(4 * core + i // 4 != b)
        def _():
            hid_copy(i, 0).wait_send()

        @pl.when(i > 0)
        def _():
            remote(zsend.at[i], zrecv.at[i], s_z.at[i], r_z.at[i], z_dev(1), b).wait_send()
            remote(pri.at[z], pri.at[z], s_g.at[i], r_g.at[i], z_dev(1), b).wait_send()
            t_copy(i).wait_send()

        return c

    lax.fori_loop(0, NZ, drain, 0)
    for i in range(4):
        for j in (1, 2, 3):
            u_copy(i, j).wait_send()

        @pl.when(4 * core + i != b)
        def _():
            u_copy(i, 0).wait_send()


def body(posterior, transition, emission, advance, dfa_state, edge_next, token_edge, allowed):
    vm = pl.BlockSpec(memory_space=pltpu.VMEM)
    dma = pltpu.SemaphoreType.DMA
    return pl.pallas_call(
        kernel,
        out_shape=jax.ShapeDtypeStruct((64, TK), F32),
        in_specs=[pl.BlockSpec(memory_space=pltpu.HBM)] * 8,
        out_specs=vm,
        scratch_shapes=[
            pltpu.VMEM((512, 256), BF),
            pltpu.VMEM((256, 2 * KC), BF),
            pltpu.VMEM((256, KC), BF),
            pltpu.VMEM((1, 512), jnp.int32),
            pltpu.VMEM((8, 256), jnp.int32),
            pltpu.VMEM((256, TK), jnp.int32),
            pltpu.VMEM((2, 512), jnp.int32),
            pltpu.VMEM((2, HALF, KC), BF),
            pltpu.VMEM((2, HALF, KC), BF),
            pltpu.VMEM((2, HALF, KC), F32),
            pltpu.VMEM((NZ, CH, KC), BF),
            pltpu.VMEM((NZ, CH, KC), BF),
            pltpu.VMEM((NZ, CH, KC), BF),
            pltpu.VMEM((NZ, CH, KC), BF),
            pltpu.VMEM((2, CH, KC), F32),
            pltpu.VMEM((NZ, CH, KC), BF),
            pltpu.VMEM((4, KC, TK), BF),
            pltpu.VMEM((4, HALF + 16, TK), BF),
            pltpu.VMEM((4, HALF, TK), BF),
            pltpu.VMEM((8, NZ, CH, KC), BF),
            pltpu.VMEM((HALF, KC), BF),
            pltpu.VMEM((4, HALF, TK), F32),
            pltpu.VMEM((NZ, 4, CH, TK), BF),
            pltpu.VMEM((16, 64, TK), BF),
            pltpu.VMEM((2, 128), F32),
            pltpu.VMEM((NZ, 2, 128), F32),
            pltpu.VMEM((2, 1, 128), F32),
            pltpu.VMEM((16, 1, 128), F32),
            pltpu.VMEM((HALF, 128), F32),
            pltpu.VMEM((64, TK), F32),
            pltpu.VMEM((HALF, 128), F32),
            pltpu.VMEM((HALF, 128), jnp.int32),
            pltpu.VMEM((HALF, HALF), BF),
            dma((8,)),
            dma((2,)),
            dma((2,)),
            dma((NZ,)),
            dma((NZ,)),
            dma((NZ,)),
            dma((NZ,)),
            dma((NZ,)),
            dma((NZ,)),
            dma((9,)),
            dma((9,)),
            dma((3,)),
            dma((3,)),
            dma((NZ, 4)),
            dma((16,)),
            dma((NZ,)),
            dma((NZ,)),
            dma((4, 4)),
            dma((16,)),
        ],
        compiler_params=pltpu.CompilerParams(
            collective_id=0, has_side_effects=True, vmem_limit_bytes=62 * 1024 * 1024
        ),
        name="constrained",
    )(
        posterior,
        transition,
        emission,
        advance,
        dfa_state.reshape(1, 512),
        edge_next.T,
        token_edge,
        allowed.T,
    )


def solution(mesh):
    in_specs = (
        P(None, "vocab"),
        P("vocab", "hid"),
        P("hid", "vocab"),
        P(None, "hid"),
        P(),
        P(),
        P(None, "vocab"),
        P(None, "vocab"),
    )
    out_specs = P("hid", "vocab")
    return jax.shard_map(body, mesh=mesh, in_specs=in_specs, out_specs=out_specs, check_vma=False)
```

```python
import jax
import jax.numpy as jnp
from jax import lax
from jax.experimental import pallas as pl
from jax.experimental.pallas import tpu as pltpu
from jax.sharding import PartitionSpec as P

MESH = pl.DeviceIdType.MESH
BF = jnp.bfloat16
F32 = jnp.float32
NZ = 16
CH = 16
HALF = 256
KC = 1024
TK = 256
TARGET = {
    -4: 1, -6: -1, -7: -2, 8: -3, 4: -1, 6: 1, 7: 2,
    1: 1, -1: -1, 2: 2, -2: -2, 3: 3, -3: -3, 5: 5, -5: -5,
}
FIRST = (8, -7, 7, -4, 4, -6, 6)
X_ORDER = FIRST + (-5, 5, -3, 3, -2, 2, -1, 1, 0)
BARRIER_STEPS = (3, -3, 2, -2, 1, -1)
EB = 4
ER = KC // EB


def remote(src, dst, send, recv, a, b):
    return pltpu.make_async_remote_copy(
        src_ref=src,
        dst_ref=dst,
        send_sem=send,
        recv_sem=recv,
        device_id={"vocab": a, "hid": b},
        device_id_type=MESH,
    )


def kernel(
    post_h,
    trans_h,
    em_h,
    adv_h,
    dfa_h,
    edge_h,
    tedge_h,
    allow_h,
    out,
    post,
    trans,
    adv,
    dfa,
    edge,
    tedge,
    allow,
    csend,
    crecv,
    own,
    xsend,
    xrecv,
    zsend,
    zrecv,
    agg,
    pri,
    em4,
    tab4,
    te4,
    gath,
    wbuf,
    cand,
    hsend,
    hrecv,
    tsend,
    trecv,
    usend,
    urecv,
    tcol,
    logs,
    allowed_rows,
    suc,
    hot,
    l_in,
    s_c,
    r_c,
    s_x,
    r_x,
    s_z,
    r_z,
    s_g,
    r_g,
    s_e,
    r_e,
    s_t,
    r_t,
    s_h,
    r_h,
    s_s,
    r_s,
    s_u,
    r_u,
):
    a = lax.axis_index("vocab")
    b = lax.axis_index("hid")
    z = a // 4
    q = lax.rem(a, 4)
    xl = q // 2
    core = lax.rem(q, 2)
    ocore = 1 - core
    oxl = 1 - xl
    a_core = 4 * z + 2 * xl + ocore
    a_x = 4 * z + 2 * oxl + core

    half_rows = pl.ds(pl.multiple_of(xl * KC, KC), KC)
    loads = [
        pltpu.make_async_copy(post_h, post, l_in.at[0]),
        pltpu.make_async_copy(trans_h, trans, l_in.at[1]),
        pltpu.make_async_copy(tedge_h, tedge, l_in.at[2]),
        pltpu.make_async_copy(allow_h, allow, l_in.at[3]),
        pltpu.make_async_copy(dfa_h, dfa, l_in.at[4]),
        pltpu.make_async_copy(edge_h, edge, l_in.at[5]),
        pltpu.make_async_copy(adv_h.at[:, half_rows], adv, l_in.at[6]),
        pltpu.make_async_copy(em_h.at[half_rows, :], em4.at[0], l_in.at[7]),
    ]
    for cp in loads:
        cp.start()

    def zmod(v):
        return lax.rem(v + 2 * NZ, NZ)

    def z_dev(step):
        return 4 * zmod(z + step) + q

    bar = pltpu.get_barrier_semaphore()

    def sig_group(i, c):
        m = lax.rem(q * 8 + b + i, 32)
        pl.semaphore_signal(
            bar, inc=1, device_id={"vocab": 4 * z + m // 8, "hid": lax.rem(m, 8)}, device_id_type=MESH
        )
        return c

    for step in BARRIER_STEPS:
        pl.semaphore_signal(bar, inc=1, device_id={"vocab": z_dev(step), "hid": b}, device_id_type=MESH)
    lax.fori_loop(1, 32, sig_group, 0)

    def part(row_half, col_half):
        rows = pl.ds(pl.multiple_of(row_half * HALF, HALF), HALF)
        cols = pl.ds(pl.multiple_of(col_half * KC, KC), KC)
        return jnp.dot(post[rows, :], trans[:, cols], preferred_element_type=F32)

    loads[0].wait()
    loads[1].wait()
    csend[0] = part(ocore, oxl).astype(BF)
    pl.semaphore_wait(bar, 31 + len(BARRIER_STEPS))

    def c_copy(zc):
        rows = pl.ds(pl.multiple_of(zc * CH, CH), CH)
        return remote(csend.at[0, rows, :], crecv.at[0, rows, :], s_c.at[zc], r_c.at[zc], a_core, b)

    for o in X_ORDER:
        c_copy(zmod(z + o)).start()

    def e_copy(i):
        rows = pl.ds(pl.multiple_of(oxl * KC + i * ER, ER), ER)
        return remote(em_h.at[rows, :], em4.at[2, pl.ds(i * ER, ER), :], s_e.at[1 + i], r_e.at[1 + i], a_x, b)

    def f_copy(i):
        rows = pl.ds(i * ER, ER)
        return remote(em4.at[2, rows, :], em4.at[3, rows, :], s_e.at[5 + i], r_e.at[5 + i], a_core, b)

    e_copy(0).start()
    csend[1] = part(ocore, xl).astype(BF)
    c1 = remote(csend.at[1], crecv.at[1], s_c.at[NZ], r_c.at[NZ], a_core, b)
    c1.start()

    loads[2].wait()
    loads[3].wait()
    tab4[0, pl.ds(0, HALF), :] = tedge[...].astype(F32).astype(BF)
    al = allow[...].astype(F32)
    al_rows = jnp.concatenate([al[:, :HALF], al[:, HALF:], jnp.zeros((12, HALF), F32)], axis=0)
    tab4[0, pl.ds(HALF, 16), :] = al_rows.astype(BF)
    t_core = remote(tab4.at[0], tab4.at[1], s_t.at[0], r_t.at[0], a_core, b)
    t_x = remote(tab4.at[0], tab4.at[2], s_t.at[1], r_t.at[1], a_x, b)
    t_core.start()

    own[0] = part(core, oxl)

    def x_copy(zc):
        return remote(xsend.at[zc], xrecv.at[zc], s_x.at[zc], r_x.at[zc], a_x, b)

    for o in X_ORDER:
        zc = zmod(z + o)
        rows = pl.ds(pl.multiple_of(zc * CH, CH), CH)
        c_copy(zc).wait_recv()
        xsend[zc] = (own[0, rows, :] + crecv[0, rows, :].astype(F32)).astype(BF)
        x_copy(zc).start()
    e_core = remote(em_h.at[half_rows, :], em4.at[1], s_e.at[0], r_e.at[0], a_core, b)
    e_core.start()
    own[1] = part(core, xl)

    for i in (4, 5, 6):
        loads[i].wait()
    iota_s = lax.broadcasted_iota(jnp.int32, (HALF, HALF), 0)
    iota_l = lax.broadcasted_iota(jnp.int32, (HALF, HALF), 1)
    lanes = pl.ds(pl.multiple_of(core * HALF, HALF), HALF)
    hot_t = jnp.where(iota_s == dfa[:, lanes], 1.0, 0.0).astype(F32)
    suc_t = jnp.dot(edge[...].astype(F32).astype(BF), hot_t.astype(BF), preferred_element_type=F32)
    suc[...] = jnp.transpose(jnp.concatenate([suc_t, jnp.zeros((120, HALF), F32)], axis=0)).astype(jnp.int32)
    hot[...] = jnp.transpose(hot_t).astype(BF)

    def gather(k):
        hot2 = jnp.where(iota_l == suc[:, pl.ds(k, 1)], 1.0, 0.0).astype(F32).astype(BF)
        g = jnp.dot(hot2, adv[...], preferred_element_type=F32).astype(BF)
        gath[k] = g.reshape(NZ, CH, KC)

    gather(0)
    gather(1)
    c1.wait_recv()

    def reduced(o):
        zc = zmod(z + o)
        rows = pl.ds(pl.multiple_of(zc * CH, CH), CH)
        x_copy(zc).wait_recv()
        return own[1, rows, :] + crecv[1, rows, :].astype(F32) + xrecv[zc].astype(F32)

    def z_copy(o):
        i = o % NZ
        return remote(zsend.at[i], zrecv.at[i], s_z.at[i], r_z.at[i], z_dev(TARGET[o]), b)

    def z_send(o, value):
        zsend[o % NZ] = value.astype(BF)
        z_copy(o).start()

    def z_take(o):
        z_copy(o).wait_recv()
        return zrecv[o % NZ].astype(F32)

    for k, o in enumerate(FIRST):
        z_send(o, reduced(o))
        if k < 6:
            gather(k + 2)
    low = reduced(-5)
    for o in (8, -7, -4, -6):
        low = low + z_take(o)
    agg[0] = low
    high = reduced(5)
    for o in (7, 4, 6):
        high = high + z_take(o)
    z_send(-5, agg[0])
    z_send(5, high)
    t_x.start()
    for i in range(1, EB):
        e_copy(i).start()
    for o in (-3, 3, -2, 2, -1, 1):
        z_send(o, reduced(o))
    agg[0] = reduced(0)
    e_copy(0).wait_recv()
    f_copy(0).start()
    t_x.wait_recv()
    t_f = remote(tab4.at[2], tab4.at[3], s_t.at[2], r_t.at[2], a_core, b)
    t_f.start()

    total = agg[0]
    for o in (-1, 1, -2, 2, -3, 3, -5, 5):
        total = total + z_take(o)
    pri[z] = total.astype(BF)

    def g_copy(chunk, step, o, part_of=None):
        ref = pri.at[zmod(z + chunk)]
        if part_of is not None:
            ref = ref.at[:, pl.ds(part_of * (KC // 2), KC // 2)]
        i = o % NZ
        h = part_of or 0
        return remote(ref, ref, s_g.at[i, h], r_g.at[i, h], z_dev(step), b)

    for h in range(2):
        for step in (5, -5):
            g_copy(0, step, -step, h).start()

    t_core.wait_recv()
    t_f.wait_recv()
    for j in range(4):
        te = jnp.dot(hot[...], tab4[j, pl.ds(0, HALF), :], preferred_element_type=F32)
        al = tab4[j, pl.ds(HALF, 16), :].astype(F32)
        al = jnp.where(core == 0, al[0:2], al[2:4])
        al_t = jnp.transpose(jnp.concatenate([al, jnp.zeros((126, HALF), F32)], axis=0))
        ok = jnp.where(iota_l < 128, al_t[:, 0:1], al_t[:, 1:2])
        te4[j] = jnp.where(ok > 0.0, te, 8.0).astype(BF)
    for step in (3, -3, 2, -2, 1, -1):
        g_copy(0, step, -step).start()

    src = xl * 8 + b

    def hid_copy(zc, j):
        qa = [q, 2 * xl + ocore, 2 * oxl + core, 2 * oxl + ocore][j]
        dst = hrecv.at[src, pl.ds(pl.multiple_of(lax.rem(zc, 4) * CH, CH), CH), :]
        return remote(hsend.at[zc, j], dst, s_h.at[zc, j], r_h.at[src], 4 * z + qa, 4 * core + zc // 4)

    def hid_local(zc):
        dst = hrecv.at[src, pl.ds(pl.multiple_of(lax.rem(zc, 4) * CH, CH), CH), :]
        return pltpu.make_async_copy(hsend.at[zc, 0], dst, r_h.at[src])

    def pri_wait(o):
        zc = zmod(z + o)
        remote(pri.at[zc], pri.at[zc], s_g.at[zmod(o), 0], r_g.at[zmod(o), 0], z_dev(1), b).wait_recv()

    def pri_wait_half(o, h):
        ref = pri.at[zmod(z + o), :, pl.ds(h * (KC // 2), KC // 2)]
        remote(ref, ref, s_g.at[zmod(o), h], r_g.at[zmod(o), h], z_dev(1), b).wait_recv()

    def score(t, c):
        m = jnp.where(t == 3, 5, jnp.where(t == 4, 4, t + 1))
        o0 = jnp.where(t == 7, 0, -m)
        zc0 = zmod(z + o0)
        zc1 = zmod(z + m)

        @pl.when(t < 3)
        def _():
            pri_wait(o0)
            pri_wait(m)

        @pl.when(t > 3)
        def _():
            pri_wait_half(m, 0)
            pri_wait_half(m, 1)

        @pl.when(jnp.logical_and(t > 3, t < 7))
        def _():
            pri_wait_half(o0, 0)
            pri_wait_half(o0, 1)

        x0 = pri[zc0]
        x1 = pri[zc1]
        for k in range(8):
            wbuf[pl.ds(k * 2 * CH, CH), :] = gath[k, zc0] * x0
            wbuf[pl.ds(k * 2 * CH + CH, CH), :] = gath[k, zc1] * x1
        for j in range(4):
            cand[j] = jnp.dot(wbuf[...], em4[j], preferred_element_type=F32)
        tot = jnp.zeros((2 * CH, 1), F32)
        for j in range(4):
            te = jnp.concatenate(
                [
                    te4[j, pl.ds(pl.multiple_of(zc0 * CH, CH), CH), :],
                    te4[j, pl.ds(pl.multiple_of(zc1 * CH, CH), CH), :],
                ],
                axis=0,
            ).astype(F32)
            chosen = jnp.zeros((2 * CH, TK), F32)
            for k in range(8):
                chosen = jnp.where(te == float(k), cand[j, pl.ds(k * 2 * CH, 2 * CH), :], chosen)
            tot = tot + jnp.sum(chosen, axis=1, keepdims=True)
            picked = chosen.astype(BF)
            hsend[zc0, j] = picked[:CH]
            hsend[zc1, j] = picked[CH:]
        wide = jnp.broadcast_to(tot, (2 * CH, 128))
        tcol[pl.ds(pl.multiple_of(zc0 * CH, CH), CH), :] = wide[:CH]
        tcol[pl.ds(pl.multiple_of(zc1 * CH, CH), CH), :] = wide[CH:]
        for zc in (zc0, zc1):
            for j in (3, 2, 1):
                hid_copy(zc, j).start()
            mine = 4 * core + zc // 4 == b

            @pl.when(mine)
            def _():
                hid_local(zc).start()

            @pl.when(jnp.logical_not(mine))
            def _():
                hid_copy(zc, 0).start()

        @pl.when(t == 0)
        def _():
            for h in range(2):
                pri_wait_half(-5, h)
                for step in (3, 2, -1, 1):
                    g_copy(-5, step, -5 - step, h).start()
                pri_wait_half(5, h)
                for step in (-2, 1, -1):
                    g_copy(5, step, 5 - step, h).start()

        return c

    loads[7].wait()
    e_core.wait_recv()
    for i in range(1, EB):
        e_copy(i).wait_recv()
        f_copy(i).start()
    for i in range(EB):
        f_copy(i).wait_recv()
    lax.fori_loop(0, NZ // 2, score, 0)

    tsend[0:1] = jnp.transpose(tcol[pl.ds(0, 128), :])[0:1]
    tsend[1:2] = jnp.transpose(tcol[pl.ds(128, 128), :])[0:1]

    def t_copy(i):
        d = zmod(i)
        return remote(tsend, trecv.at[d], s_s.at[d], r_s.at[d], z_dev(i), b)

    def t_step(i, c):
        t_copy(lax.rem(i + 7, 15) + 1).start()
        return c

    lax.fori_loop(0, NZ - 1, t_step, 0)
    trecv[0] = tsend[...]

    def h_wait(i, c):
        remote(hrecv.at[i], hrecv.at[i], s_h.at[0, 0], r_h.at[i], a_core, b).wait_recv()
        return c

    lax.fori_loop(0, 16, h_wait, 0)
    scores = jnp.zeros((64, TK), F32)
    for i in range(16):
        scores = scores + hrecv[i].astype(F32)
    al = tab4[0, pl.ds(HALF, 16), :].astype(F32)
    al = jnp.where(b < 4, al[0:2], al[2:4])
    al_t = jnp.transpose(jnp.concatenate([al, jnp.zeros((126, HALF), F32)], axis=0))
    allowed_rows[...] = al_t
    al_t = allowed_rows[pl.ds(pl.multiple_of(lax.rem(b, 4) * 64, 64), 64), :]
    lane_v = lax.broadcasted_iota(jnp.int32, (64, TK), 1)
    mask = jnp.where(lane_v < 128, al_t[:, 0:1], al_t[:, 1:2]) > 0.0
    logs[...] = jnp.log(jnp.where(mask, scores, 1.0))

    def t_wait(i, c):
        t_copy(i).wait_recv()
        return c

    lax.fori_loop(1, NZ, t_wait, 0)
    part_tot = trecv[0]
    for d in range(1, NZ):
        part_tot = part_tot + trecv[d]
    usend[0] = part_tot[0:1]
    usend[1] = part_tot[1:2]

    def u_copy(i, j):
        qa = [q, 2 * xl + ocore, 2 * oxl + core, 2 * oxl + ocore][j]
        return remote(usend.at[i // 2], urecv.at[src], s_u.at[i, j], r_u.at[src], 4 * z + qa, 4 * core + i)

    for i in range(4):
        for j in (3, 2, 1):
            u_copy(i, j).start()
        mine = 4 * core + i == b

        @pl.when(mine)
        def _():
            pltpu.make_async_copy(usend.at[i // 2], urecv.at[src], r_u.at[src]).start()

        @pl.when(jnp.logical_not(mine))
        def _():
            u_copy(i, 0).start()

    for cp in (c1, e_core, t_core, t_x, t_f):
        cp.wait_send()
    for i in range(EB):
        e_copy(i).wait_send()
        f_copy(i).wait_send()

    def drain(i, c):
        x_copy(i).wait_send()
        c_copy(i).wait_send()
        for j in (1, 2, 3):
            hid_copy(i, j).wait_send()

        @pl.when(4 * core + i // 4 != b)
        def _():
            hid_copy(i, 0).wait_send()

        @pl.when(i > 0)
        def _():
            remote(zsend.at[i], zrecv.at[i], s_z.at[i], r_z.at[i], z_dev(1), b).wait_send()
            t_copy(i).wait_send()

        return c

    lax.fori_loop(0, NZ, drain, 0)
    for o in (1, 2, 3, -1, -2, -3):
        g_copy(0, 1, o).wait_send()
    for o in (4, 5, 6, 7, 8, -4, -5, -6, -7):
        for h in range(2):
            g_copy(0, 1, o, h).wait_send()

    def u_wait(i, c):
        remote(urecv.at[i], urecv.at[i], s_u.at[0, 0], r_u.at[i], a_core, b).wait_recv()
        return c

    lax.fori_loop(0, 16, u_wait, 0)
    full = urecv[0]
    for i in range(1, 16):
        full = full + urecv[i]
    column = jnp.transpose(jnp.broadcast_to(full, (128, 128)))
    column = jnp.where(lax.rem(b, 2) == 0, column[:64, 0:1], column[64:, 0:1])
    out[...] = jnp.where(mask, logs[...] - jnp.log(column), 0.0)
    for i in range(4):
        for j in (1, 2, 3):
            u_copy(i, j).wait_send()

        @pl.when(4 * core + i != b)
        def _():
            u_copy(i, 0).wait_send()


def body(posterior, transition, emission, advance, dfa_state, edge_next, token_edge, allowed):
    vm = pl.BlockSpec(memory_space=pltpu.VMEM)
    dma = pltpu.SemaphoreType.DMA
    return pl.pallas_call(
        kernel,
        out_shape=jax.ShapeDtypeStruct((64, TK), F32),
        in_specs=[pl.BlockSpec(memory_space=pltpu.HBM)] * 8,
        out_specs=vm,
        scratch_shapes=[
            pltpu.VMEM((512, 256), BF),
            pltpu.VMEM((256, 2 * KC), BF),
            pltpu.VMEM((256, KC), BF),
            pltpu.VMEM((1, 512), jnp.int32),
            pltpu.VMEM((8, 256), jnp.int32),
            pltpu.VMEM((256, TK), jnp.int32),
            pltpu.VMEM((2, 512), jnp.int32),
            pltpu.VMEM((2, HALF, KC), BF),
            pltpu.VMEM((2, HALF, KC), BF),
            pltpu.VMEM((2, HALF, KC), F32),
            pltpu.VMEM((NZ, CH, KC), BF),
            pltpu.VMEM((NZ, CH, KC), BF),
            pltpu.VMEM((NZ, CH, KC), BF),
            pltpu.VMEM((NZ, CH, KC), BF),
            pltpu.VMEM((2, CH, KC), F32),
            pltpu.VMEM((NZ, CH, KC), BF),
            pltpu.VMEM((4, KC, TK), BF),
            pltpu.VMEM((4, HALF + 16, TK), BF),
            pltpu.VMEM((4, HALF, TK), BF),
            pltpu.VMEM((8, NZ, CH, KC), BF),
            pltpu.VMEM((HALF, KC), BF),
            pltpu.VMEM((4, HALF, TK), F32),
            pltpu.VMEM((NZ, 4, CH, TK), BF),
            pltpu.VMEM((16, 64, TK), BF),
            pltpu.VMEM((2, 128), F32),
            pltpu.VMEM((NZ, 2, 128), F32),
            pltpu.VMEM((2, 1, 128), F32),
            pltpu.VMEM((16, 1, 128), F32),
            pltpu.VMEM((HALF, 128), F32),
            pltpu.VMEM((64, TK), F32),
            pltpu.VMEM((HALF, 128), F32),
            pltpu.VMEM((HALF, 128), jnp.int32),
            pltpu.VMEM((HALF, HALF), BF),
            dma((8,)),
            dma((NZ + 1,)),
            dma((NZ + 1,)),
            dma((NZ,)),
            dma((NZ,)),
            dma((NZ,)),
            dma((NZ,)),
            dma((NZ, 2)),
            dma((NZ, 2)),
            dma((9,)),
            dma((9,)),
            dma((3,)),
            dma((3,)),
            dma((NZ, 4)),
            dma((16,)),
            dma((NZ,)),
            dma((NZ,)),
            dma((4, 4)),
            dma((16,)),
        ],
        compiler_params=pltpu.CompilerParams(
            collective_id=0, has_side_effects=True, vmem_limit_bytes=62 * 1024 * 1024
        ),
        name="constrained",
    )(
        posterior,
        transition,
        emission,
        advance,
        dfa_state.reshape(1, 512),
        edge_next.T,
        token_edge,
        allowed.T,
    )


def solution(mesh):
    in_specs = (
        P(None, "vocab"),
        P("vocab", "hid"),
        P("hid", "vocab"),
        P(None, "hid"),
        P(),
        P(),
        P(None, "vocab"),
        P(None, "vocab"),
    )
    out_specs = P("hid", "vocab")
    return jax.shard_map(body, mesh=mesh, in_specs=in_specs, out_specs=out_specs, check_vma=False)
```
